768 devices in a mesh: dp: 128 (over x, z_hi, y, core), tensor: 6 (over z_lo).
Axes of the slice: x: 4, y: 8, z: 12 (z_hi: 2, z_lo: 6; z = z_hi * 6 + z_lo), core: 2. Of those that a mesh axis runs over, the one named last changes fastest.
Arguments:
- resid: bfloat16 [512, 32, 8192], P('dp'), may hold values from -24 to 24
- norm_gain: float32 [8192], replicated, may hold values from 0.1 to 1.9
- w_value: bfloat16 [8192, 768], P('dp', 'tensor'), may hold values from -0.0625 to 0.0625
- d_value: bfloat16 [512, 32, 768], P('dp', None, 'tensor'), may hold values from -6 to 6
- rewards: bfloat16 [512], P('dp'), may hold values from 0 to 1
- lengths: int32 [128, 4], P('dp'), may hold values from 1 to 32, 96 in all within a row
Outputs:
- value: bfloat16 [512, 32, 768], P('dp', None, 'tensor')
- w_grad: bfloat16 [8192, 768], P('dp', 'tensor')
The draws below stay inside these ranges and needn't reach their ends.
Inputs may be any that keep to these rules, and one draw needn't show every extreme that they name: The 4 responses of each index of dp have lengths that sum to exactly 96.
All inputs are finite; a program needn't handle non-finite values.
Results may differ from the reference program's by a relative error of at most 0.0058.
Values may be sent and summed in bfloat16 or wider, within the bound.
No kernel may reach another device: no remote copies, remote signals or barrier semaphores. Data moves between devices by JAX's collectives and lax.ppermute only.
A program may use at most 32 MiB of HBM per device.

```python
import math
import jax
import jax.numpy as jnp
import numpy as np
from jax import lax

D = 8192
HV = 768
RPD = 4
SLOTS = 32
GROUP = 16
ROWS_DP = 96
ROLL = 512
N_DP = 128


def with_spikes(values, own_key, source, target, shards_of, factor):
    def block_of(axis_at):
        return (jnp.arange(values.shape[axis_at]) // (values.shape[axis_at] // shards_of)).reshape((-1,) + (1,) * (values.ndim - 1 - axis_at))

    first = jax.random.permutation(own_key, shards_of)[block_of(target)]
    other_side = (block_of(target) + shards_of // 2) % shards_of
    return jnp.where((block_of(source) == first) | (block_of(source) == other_side), factor * values, values)


def level_of(rng, shape, cuts, smallest, high):
    def one(dim, blocks):
        draws = jax.random.uniform(jax.random.fold_in(jax.random.fold_in(rng, 6), dim), (blocks,), jnp.float32, smallest / len(cuts), high / len(cuts))
        return jnp.repeat(jnp.exp(draws), shape[dim] // blocks).reshape((-1,) + (1,) * (len(shape) - dim - 1))

    factor_of = one(*cuts[0])
    for cut in cuts[1:]:
        factor_of = factor_of * one(*cut)
    return factor_of


def length_profile(number_of, total, bound, slope):
    portions = [(1 << 20) // math.isqrt(standing ** slope) + 1 for standing in range(2, number_of + 1)]
    surplus, given = total - bound - (number_of - 1), [1] * (number_of - 1)
    while surplus > 0:
        candidates = [i for i in range(number_of - 1) if given[i] < bound]
        whole, budget = sum([portions[i] for i in candidates]), surplus
        for i in candidates:
            addition = min(bound - given[i], max(1, budget * portions[i] // whole), surplus)
            given[i] = given[i] + addition
            surplus = surplus - addition
    return np.array([bound] + given)


def ragged(rng, number_of, total, reach, skew):
    if number_of == 2:
        one = jax.random.randint(rng, (), max(1, total - reach), min(reach, total - 1) + 1)
        return jnp.stack([one, total - one])
    tallies = jnp.asarray(length_profile(number_of, total, reach, skew), jnp.int32)
    pairs = (number_of - 1) // 2
    giver, taker = tallies[1:1 + 2 * pairs:2], tallies[2:2 + 2 * pairs:2]
    slack = jnp.minimum(giver - 1, reach - taker)
    shifted = jax.random.randint(jax.random.fold_in(rng, 1), (pairs,), 0, 1 << 20) % (slack + 1)
    tallies = tallies.at[1:1 + 2 * pairs:2].set(giver - shifted).at[2:2 + 2 * pairs:2].set(taker + shifted)
    return tallies[jax.random.permutation(jax.random.fold_in(rng, 2), number_of)]


def scatter_about(rng, dims, scale, bound, split=(), held_as=jnp.bfloat16):
    level = level_of(rng, dims, split, -0.22, 0.18) if split else 1.0
    entries = jax.random.normal(rng, dims, jnp.float32) * scale * level
    return jnp.minimum(jnp.maximum(entries, -bound), bound).astype(held_as)


def noise_with(own_key, dims, spread, reach, pieces, heavy, held_as=jnp.bfloat16):
    drawn = spread * jax.random.normal(own_key, dims, jnp.float32)
    if pieces:
        drawn = drawn * level_of(own_key, dims, pieces, -0.22, 0.18)
    return jnp.clip(with_spikes(drawn, jax.random.fold_in(own_key, 3), *heavy), -reach, reach).astype(held_as)


def setup_inputs(seed: int = 0) -> dict:
    streams_of = jax.random.split(jax.random.key(seed), 7)
    resid = noise_with(streams_of[0], (ROLL, SLOTS, D), 1.0, 24.0, ((0, 128),), (0, 2, 128, 5.5))
    norm_gain = jnp.clip(1.0 + 0.18 * jax.random.normal(streams_of[1], (D,), jnp.float32), 0.1, 1.9)
    w_value = scatter_about(streams_of[2], (D, HV), D ** -0.5, 0.0625, ((0, 128), (1, 6)))
    d_value = scatter_about(streams_of[3], (ROLL, SLOTS, HV), 1.0, 6.0, ((0, 128), (2, 6)))
    rewards = jnp.clip(1.0 * jax.random.uniform(streams_of[4], (ROLL,), jnp.float32) ** level_of(streams_of[4], (ROLL,), ((0, 128),), -0.2, 0.2), 0.0, 1.0).astype(jnp.bfloat16)
    lengths = jax.vmap(lambda own: ragged(own, RPD, ROWS_DP, SLOTS, 0))(jax.random.split(streams_of[5], N_DP)).reshape((N_DP, RPD)).astype(jnp.int32)
    return {"resid": resid, "norm_gain": norm_gain, "w_value": w_value, "d_value": d_value, "rewards": rewards, "lengths": lengths}


def reference(resid, norm_gain, w_value, d_value, rewards, lengths):
    roll_len = lengths.reshape(ROLL).astype(jnp.int32)
    reward_grid = rewards.astype(jnp.float32).reshape(ROLL // GROUP, GROUP)
    group_mean = lax.optimization_barrier(jnp.mean(reward_grid, axis=1, keepdims=True))
    group_spread = jnp.sqrt(lax.optimization_barrier(jnp.mean((reward_grid - group_mean) ** 2, axis=1, keepdims=True)))
    advantage = ((reward_grid - group_mean) / jnp.maximum(group_spread, 0.25)).reshape(ROLL)
    coef_roll = -advantage / roll_len.astype(jnp.float32)
    live_grid = (jnp.arange(SLOTS, dtype=jnp.int32)[None, :] < roll_len[:, None]).astype(jnp.float32)
    block_count = ROLL // GROUP
    resid_blocks = resid.reshape(block_count, GROUP * SLOTS, D)
    dval_blocks = d_value.reshape(block_count, GROUP * SLOTS, HV)
    live_blocks = live_grid.reshape(block_count, GROUP * SLOTS)
    coef_blocks = jnp.repeat(coef_roll, SLOTS).reshape(block_count, GROUP * SLOTS)

    def step_block(running, inputs):
        resid_rows, dval_rows, live_mask, row_coef = inputs
        states = resid_rows.astype(jnp.float32)
        mean_sq = lax.optimization_barrier(jnp.mean(states * states, axis=-1, keepdims=True))
        normed = (states * lax.rsqrt(mean_sq + 1e-05) * norm_gain).astype(jnp.bfloat16)
        value_rows = (jnp.dot(normed, w_value, preferred_element_type=jnp.float32) * live_mask[:, None]).astype(jnp.bfloat16)
        dscaled = (dval_rows.astype(jnp.float32) * (row_coef * live_mask)[:, None]).astype(jnp.bfloat16)
        running = running + jnp.dot(normed.T, dscaled, preferred_element_type=jnp.float32)
        return (running, value_rows)
    start_grad = jnp.zeros((D, HV), jnp.float32)
    grad_total, value_blocks = lax.scan(step_block, start_grad, (resid_blocks, dval_blocks, live_blocks, coef_blocks))
    value = value_blocks.reshape(ROLL, SLOTS, HV)
    return (value, grad_total.astype(jnp.bfloat16))
```

```python
import jax
import jax.numpy as jnp
from jax import lax
from jax.sharding import Mesh
from jax.sharding import PartitionSpec as P

DP = ("x", "zh", "y", "c")
SWAP = ((0, 1), (1, 0))
Y_PAIR = tuple((j, j ^ 1) for j in range(8))
STRAIGHT = tuple((2 * z + c, 2 * c + z) for z in range(2) for c in range(2))
CROSSED = tuple((2 * z + c, 2 * c + 1 - z) for z in range(2) for c in range(2))
CROSSED_BACK = tuple((b, a) for a, b in CROSSED)


def per_device(resid, norm_gain, w_value, d_value, rewards, lengths):
    bf, f32 = jnp.bfloat16, jnp.float32
    rolls, slots, width = resid.shape
    rows = rolls * slots
    cols = w_value.shape[1]
    nx, nz, ny, nc = [lax.axis_size(a) for a in DP]
    core = lax.axis_index("c")
    zpart = lax.axis_index("zh")
    chunk = width // nx // nz
    half = nx * chunk

    w_a = lax.ppermute(w_value, ("zh", "c"), STRAIGHT)
    w_b = lax.ppermute(w_value, ("zh", "c"), CROSSED_BACK)
    near_rewards = lax.ppermute(rewards, "y", Y_PAIR)

    x = resid.reshape(rows, width)
    states = x.astype(f32)
    scale = lax.rsqrt(jnp.mean(states * states, axis=-1, keepdims=True) + 1e-5)
    normed = (states * scale * norm_gain).astype(bf)
    pieces = [normed[:, k * chunk : (k + 1) * chunk] for k in range(nx * nz)]

    def part(which):
        return jnp.concatenate([jnp.where(which == 0, a, b) for a, b in zip(pieces[::2], pieces[1::2])], axis=1)

    own = part(core)
    dval = d_value.reshape(rows, cols)
    small = jnp.concatenate([rewards, near_rewards, lengths.reshape(rolls).astype(bf)])
    small = jnp.broadcast_to(jnp.pad(small, (0, cols - 3 * rolls))[None], (8, cols))
    small = jnp.pad(small, ((0, rows - 8), (0, 0)))
    packed = jnp.concatenate([part(1 - core), dval, small], axis=1)
    packed = lax.ppermute(packed, "c", SWAP)
    other = packed[:, :half]
    dval_other = packed[:, half : half + cols]
    tail = packed[0, half + cols :].astype(f32)

    own_r = rewards.astype(f32)
    own_l = lengths.reshape(rolls).astype(f32)
    group = jnp.concatenate([own_r, near_rewards.astype(f32), tail[: 2 * rolls]])
    mean = jnp.mean(group)
    spread = jnp.maximum(jnp.sqrt(jnp.mean((group - mean) ** 2)), 0.25)

    def scaled(dv, rew, length):
        coef = -((rew - mean) / spread) / length
        place = jnp.arange(slots, dtype=jnp.int32).astype(f32)
        live = (place[None, :] < length[:, None]).astype(f32)
        factor = (coef[:, None] * live)[:, :, None]
        return (dv.reshape(rolls, slots, cols).astype(f32) * factor).astype(bf).reshape(rows, cols)

    ds_own = scaled(dval, own_r, own_l)
    ds_other = scaled(dval_other, tail[:rolls], tail[2 * rolls : 3 * rolls])
    over_rows = (((0,), (0,)), ((), ()))
    grad = lax.dot_general(own, ds_own, over_rows, preferred_element_type=f32)
    grad = grad + lax.dot_general(other, ds_other, over_rows, preferred_element_type=f32)
    nxy = nx * ny
    per = half // nxy

    w_pair = jnp.where(zpart == 0, jnp.concatenate([w_a, w_b]), jnp.concatenate([w_b, w_a]))
    send = jnp.concatenate(
        [grad.astype(bf).reshape(nxy, per, cols), jnp.broadcast_to(w_pair[None], (nxy, per, cols))], axis=1
    )
    got = lax.all_to_all(send, ("x", "y"), 0, 0, tiled=True)
    g_sum = jnp.sum(got[:, :per].astype(f32), axis=0).reshape(nc, per // nc, cols)
    g_a = lax.ppermute(jnp.where(zpart == 0, g_sum[0], g_sum[1]), ("zh", "c"), STRAIGHT)
    g_b = lax.ppermute(jnp.where(zpart == 0, g_sum[1], g_sum[0]), ("zh", "c"), CROSSED)
    w_full = got[:, per:].reshape(half, cols)
    v_other = jnp.dot(other, w_full, preferred_element_type=f32)
    v_got = lax.ppermute(v_other, "c", SWAP)
    v_own = jnp.dot(own, w_full, preferred_element_type=f32)
    live = jnp.arange(slots, dtype=jnp.int32)[None, :] < lengths.reshape(rolls, 1)
    value = (v_own + v_got).reshape(rolls, slots, cols) * live.astype(f32)[:, :, None]
    return value.astype(bf), (g_a + g_b).astype(bf)


def solution(mesh):
    finer = Mesh(mesh.devices.reshape(4, 2, 8, 2, mesh.shape["tensor"]), DP + ("tensor",))
    placed = (P(DP, None, None), P(), P(DP, "tensor"), P(DP, None, "tensor"), P(DP), P(DP, None))
    return jax.shard_map(
        per_device,
        mesh=finer,
        in_specs=placed,
        out_specs=(P(DP, None, "tensor"), P(DP, "tensor")),
        check_vma=False,
    )
```

```python
import jax
import jax.numpy as jnp
from jax import lax
from jax.experimental import pallas as pl
from jax.experimental.pallas import tpu as pltpu
from jax.sharding import Mesh
from jax.sharding import PartitionSpec as P

DP = ("x", "zh", "y", "c")
SWAP = ((0, 1), (1, 0))
Y_PAIR = tuple((j, j ^ 1) for j in range(8))
LANES = 128
BLOCK = 64
bf16, f32 = jnp.bfloat16, jnp.float32


def norm_kernel(core_ref, x_ref, gain_ref, dval_ref, rew_ref, near_ref, len_ref, own_ref, pack_ref):
    rows, width = x_ref.shape
    total = jnp.zeros((rows, LANES), f32)
    for k in range(width // LANES):
        v = x_ref[:, k * LANES : (k + 1) * LANES].astype(f32)
        total = total + v * v
    scale = lax.rsqrt(jnp.sum(total, axis=1, keepdims=True) * (1.0 / width) + 1e-5)
    first = core_ref[0] == 0
    low = lax.broadcasted_iota(jnp.int32, (rows, LANES), 1) < BLOCK
    for k in range(width // LANES // 2):
        at = 2 * k * LANES
        a = x_ref[:, at : at + LANES].astype(f32) * scale * gain_ref[:, at : at + LANES]
        b = x_ref[:, at + LANES : at + 2 * LANES].astype(f32) * scale * gain_ref[:, at + LANES : at + 2 * LANES]
        even = jnp.where(low, a, pltpu.roll(b, BLOCK, 1))
        odd = jnp.where(low, pltpu.roll(a, BLOCK, 1), b)
        own_ref[:, k * LANES : (k + 1) * LANES] = jnp.where(first, even, odd).astype(bf16)
        pack_ref[:, k * LANES : (k + 1) * LANES] = jnp.where(first, odd, even).astype(bf16)
    half = width // 2
    pack_ref[:, half : half + LANES] = dval_ref[...]
    lane = lax.broadcasted_iota(jnp.int32, (rows, LANES), 1)
    tail = jnp.zeros((rows, LANES), f32)
    n = rew_ref.shape[1]
    for s, ref in enumerate((rew_ref, near_ref, len_ref)):
        vals = ref[...].astype(f32)
        for j in range(n):
            tail = jnp.where(lane == s * n + j, vals[:, j : j + 1], tail)
    pack_ref[:, half + LANES :] = tail.astype(bf16)


def grad_kernel(own_ref, got_ref, gotd_ref, tail_ref, dval_ref, rew_ref, near_ref, len_ref, out_ref, ds_own, ds_other):
    rows, _ = dval_ref.shape
    n = rew_ref.shape[1]
    slots = rows // n

    @pl.when(pl.program_id(0) == 0)
    def _():
        rew = rew_ref[...].astype(f32)
        near = near_ref[...].astype(f32)
        tail = tail_ref[...].astype(f32)[0:1, :]
        in_group = lax.broadcasted_iota(jnp.int32, (1, LANES), 1) < 2 * n
        count = 1.0 / (4 * n)
        total = jnp.sum(rew, axis=1, keepdims=True) + jnp.sum(near, axis=1, keepdims=True)
        total = total + jnp.sum(jnp.where(in_group, tail, 0.0), axis=1, keepdims=True)
        mean = total * count
        sq = jnp.sum((rew - mean) ** 2, axis=1, keepdims=True) + jnp.sum((near - mean) ** 2, axis=1, keepdims=True)
        sq = sq + jnp.sum(jnp.where(in_group, (tail - mean) ** 2, 0.0), axis=1, keepdims=True)
        spread = jnp.maximum(jnp.sqrt(sq * count), 0.25)
        row = lax.broadcasted_iota(jnp.int32, (rows, 1), 0)
        place = (row % slots).astype(f32)

        def factor(rewards_at, length_at):
            r = jnp.zeros((rows, 1), f32)
            length = jnp.ones((rows, 1), f32)
            for j in range(n):
                mine = row // slots == j
                r = jnp.where(mine, rewards_at(j), r)
                length = jnp.where(mine, length_at(j), length)
            coef = -((r - mean) / spread) / length
            return jnp.where(place < length, coef, 0.0)

        lens = len_ref[...].astype(f32)
        own = factor(lambda j: rew[:, j : j + 1], lambda j: lens[:, j : j + 1])
        other = factor(lambda j: tail[:, j : j + 1], lambda j: tail[:, 2 * n + j : 2 * n + j + 1])
        ds_own[...] = (dval_ref[...].astype(f32) * own).astype(bf16)
        ds_other[...] = (gotd_ref[...].astype(f32) * other).astype(bf16)

    over_rows = (((0,), (0,)), ((), ()))
    acc = lax.dot_general(ds_own[...], own_ref[...], over_rows, preferred_element_type=f32)
    acc = acc + lax.dot_general(ds_other[...], got_ref[...], over_rows, preferred_element_type=f32)
    out_ref[0] = acc.astype(bf16)


def turn_kernel(got_ref, out_ref):
    total = got_ref[0].astype(f32)
    for s in range(1, got_ref.shape[0]):
        total = total + got_ref[s].astype(f32)
    for k in range(total.shape[1] // LANES):
        piece = total[:, k * LANES : (k + 1) * LANES].T.astype(bf16)
        out_ref[2 * k] = piece[:BLOCK]
        out_ref[2 * k + 1] = piece[BLOCK:]


def per_device(resid, norm_gain, w_value, d_value, rewards, lengths):
    rolls, slots, width = resid.shape
    rows = rolls * slots
    cols = w_value.shape[1]
    nx, nz, ny, nc = [lax.axis_size(a) for a in DP]
    nzy = nz * ny
    half = width // nc
    chunk = half // nx
    whole = lambda *shape: pl.BlockSpec(shape, lambda *_: (0,) * len(shape))

    near = lax.ppermute(rewards, "y", Y_PAIR)
    w_zy = lax.all_to_all(jnp.broadcast_to(w_value[None], (nzy, BLOCK, cols)), ("zh", "y"), 0, 0, tiled=True)
    w_all = lax.all_to_all(jnp.broadcast_to(w_zy[None], (nx, nzy, BLOCK, cols)), "x", 0, 0, tiled=True)
    w_full = w_all.reshape(half, cols)

    core = lax.axis_index("c").astype(jnp.int32).reshape(1)
    dval = d_value.reshape(rows, cols)
    rew, near = rewards.reshape(1, rolls), near.reshape(1, rolls)
    step = 32
    own, packed = pl.pallas_call(
        norm_kernel,
        grid=(rows // step,),
        in_specs=[
            pl.BlockSpec(memory_space=pltpu.SMEM),
            pl.BlockSpec((step, width), lambda i: (i, 0)),
            whole(1, width),
            pl.BlockSpec((step, cols), lambda i: (i, 0)),
            whole(1, rolls),
            whole(1, rolls),
            whole(1, rolls),
        ],
        out_specs=[
            pl.BlockSpec((step, half), lambda i: (i, 0)),
            pl.BlockSpec((step, half + 2 * LANES), lambda i: (i, 0)),
        ],
        out_shape=[
            jax.ShapeDtypeStruct((rows, half), bf16),
            jax.ShapeDtypeStruct((rows, half + 2 * LANES), bf16),
        ],
        name="norm_split",
    )(core, resid.reshape(rows, width), norm_gain.reshape(1, width), dval, rew, near, lengths)
    got = lax.ppermute(packed, "c", SWAP)
    send = pl.pallas_call(
        grad_kernel,
        grid=(nx,),
        in_specs=[
            pl.BlockSpec((rows, chunk), lambda k: (0, k)),
            pl.BlockSpec((rows, chunk), lambda k: (0, k)),
            pl.BlockSpec((rows, cols), lambda k: (0, half // LANES)),
            pl.BlockSpec((16, LANES), lambda k: (0, half // LANES + 1)),
            whole(rows, cols),
            whole(1, rolls),
            whole(1, rolls),
            whole(1, rolls),
        ],
        out_specs=pl.BlockSpec((1, cols, chunk), lambda k: (k, 0, 0)),
        out_shape=jax.ShapeDtypeStruct((nx, cols, chunk), bf16),
        scratch_shapes=[pltpu.VMEM((rows, cols), bf16), pltpu.VMEM((rows, cols), bf16)],
        name="grad_partial",
    )(own, got, got, got, dval, rew, near, lengths)
    g_x = lax.all_to_all(send, "x", 0, 0, tiled=True)
    split = 2
    g_send = pl.pallas_call(
        turn_kernel,
        grid=(split,),
        in_specs=[pl.BlockSpec((nx, cols, chunk // split), lambda k: (0, 0, k))],
        out_specs=pl.BlockSpec((nzy // split, BLOCK, cols), lambda k: (k, 0, 0)),
        out_shape=jax.ShapeDtypeStruct((nzy, BLOCK, cols), bf16),
        name="sum_turn",
    )(g_x)
    g_zy = lax.all_to_all(g_send, ("zh", "y"), 0, 0, tiled=True)
    w_grad = jnp.sum(g_zy.astype(f32), axis=0).astype(bf16)

    v_other = jnp.dot(got[:, :half], w_full, preferred_element_type=f32)
    v_got = lax.ppermute(v_other, "c", SWAP)
    v_own = jnp.dot(own, w_full, preferred_element_type=f32)
    live = jnp.arange(slots, dtype=jnp.int32)[None, :] < lengths.reshape(rolls, 1)
    value = (v_own + v_got).reshape(rolls, slots, cols) * live.astype(f32)[:, :, None]
    return value.astype(bf16), w_grad


def solution(mesh):
    finer = Mesh(mesh.devices.reshape(4, 2, 8, 2, mesh.shape["tensor"]), DP + ("tensor",))
    placed = (P(DP, None, None), P(), P(DP, "tensor"), P(DP, None, "tensor"), P(DP), P(DP, None))
    return jax.shard_map(
        per_device,
        mesh=finer,
        in_specs=placed,
        out_specs=(P(DP, None, "tensor"), P(DP, "tensor")),
        check_vma=False,
    )
```

```python
import jax
import jax.numpy as jnp
from jax import lax
from jax.experimental import pallas as pl
from jax.experimental.pallas import tpu as pltpu
from jax.sharding import Mesh
from jax.sharding import PartitionSpec as P

DP = ("x", "zh", "y", "c")
SWAP = ((0, 1), (1, 0))
Y_PAIR = tuple((j, j ^ 1) for j in range(8))
LANES = 128
BLOCK = 64
NX = 4
X_SHIFTS = tuple(tuple((j, (j + s) % NX) for j in range(NX)) for s in range(NX))
SWAP_Z = ((0, 1), (1, 0))
bf16, f32 = jnp.bfloat16, jnp.float32


def norm_kernel(place_ref, x_ref, gain_ref, dval_ref, rew_ref, near_ref, len_ref, own_ref, pack_ref):
    rows, width = x_ref.shape
    total = jnp.zeros((rows, LANES), f32)
    for k in range(width // LANES):
        v = x_ref[:, k * LANES : (k + 1) * LANES].astype(f32)
        total = total + v * v
    scale = lax.rsqrt(jnp.sum(total, axis=1, keepdims=True) * (1.0 / width) + 1e-5)
    first = place_ref[0] == 0
    low = lax.broadcasted_iota(jnp.int32, (rows, LANES), 1) < BLOCK
    tiles = width // LANES // 2
    for k in range(tiles):
        shift, inside = divmod(k, tiles // NX)
        at = (place_ref[1] + NX - shift) % NX * (width // NX) + inside * 2 * LANES
        at_a, at_b = pl.ds(pl.multiple_of(at, LANES), LANES), pl.ds(pl.multiple_of(at + LANES, LANES), LANES)
        a = x_ref[:, at_a].astype(f32) * scale * gain_ref[:, at_a]
        b = x_ref[:, at_b].astype(f32) * scale * gain_ref[:, at_b]
        even = jnp.where(low, a, pltpu.roll(b, BLOCK, 1))
        odd = jnp.where(low, pltpu.roll(a, BLOCK, 1), b)
        own_ref[:, k * LANES : (k + 1) * LANES] = jnp.where(first, even, odd).astype(bf16)
        pack_ref[:, k * LANES : (k + 1) * LANES] = jnp.where(first, odd, even).astype(bf16)
    half = width // 2
    pack_ref[:, half : half + LANES] = dval_ref[...]
    lane = lax.broadcasted_iota(jnp.int32, (rows, LANES), 1)
    tail = jnp.zeros((rows, LANES), f32)
    n = rew_ref.shape[1]
    for s, ref in enumerate((rew_ref, near_ref, len_ref)):
        vals = ref[...].astype(f32)
        for j in range(n):
            tail = jnp.where(lane == s * n + j, vals[:, j : j + 1], tail)
    pack_ref[:, half + LANES :] = tail.astype(bf16)


def grad_kernel(place_ref, own_ref, got_ref, gotd_ref, tail_ref, dval_ref, rew_ref, near_ref, len_ref, out_ref, ds_own, ds_other):
    rows, _ = dval_ref.shape
    n = rew_ref.shape[1]
    slots = rows // n

    @pl.when(pl.program_id(0) == 0)
    def _():
        rew = rew_ref[...].astype(f32)
        near = near_ref[...].astype(f32)
        tail = tail_ref[...].astype(f32)[0:1, :]
        in_group = lax.broadcasted_iota(jnp.int32, (1, LANES), 1) < 2 * n
        count = 1.0 / (4 * n)
        total = jnp.sum(rew, axis=1, keepdims=True) + jnp.sum(near, axis=1, keepdims=True)
        total = total + jnp.sum(jnp.where(in_group, tail, 0.0), axis=1, keepdims=True)
        mean = total * count
        sq = jnp.sum((rew - mean) ** 2, axis=1, keepdims=True) + jnp.sum((near - mean) ** 2, axis=1, keepdims=True)
        sq = sq + jnp.sum(jnp.where(in_group, (tail - mean) ** 2, 0.0), axis=1, keepdims=True)
        spread = jnp.maximum(jnp.sqrt(sq * count), 0.25)
        row = lax.broadcasted_iota(jnp.int32, (rows, 1), 0)
        place = (row % slots).astype(f32)

        def factor(rewards_at, length_at):
            r = jnp.zeros((rows, 1), f32)
            length = jnp.ones((rows, 1), f32)
            for j in range(n):
                mine = row // slots == j
                r = jnp.where(mine, rewards_at(j), r)
                length = jnp.where(mine, length_at(j), length)
            coef = -((r - mean) / spread) / length
            return jnp.where(place < length, coef, 0.0)

        lens = len_ref[...].astype(f32)
        own = factor(lambda j: rew[:, j : j + 1], lambda j: lens[:, j : j + 1])
        other = factor(lambda j: tail[:, j : j + 1], lambda j: tail[:, 2 * n + j : 2 * n + j + 1])
        ds_own[...] = (dval_ref[...].astype(f32) * own).astype(bf16)
        ds_other[...] = (gotd_ref[...].astype(f32) * other).astype(bf16)

    over_rows = (((0,), (0,)), ((), ()))
    acc = lax.dot_general(ds_own[...], own_ref[...], over_rows, preferred_element_type=f32)
    acc = acc + lax.dot_general(ds_other[...], got_ref[...], over_rows, preferred_element_type=f32)
    out_ref[0] = acc.astype(bf16)


def turn_kernel(got_ref, out_ref):
    total = got_ref[0].astype(f32)
    for s in range(1, got_ref.shape[0]):
        total = total + got_ref[s].astype(f32)
    for k in range(total.shape[1] // LANES):
        piece = total[:, k * LANES : (k + 1) * LANES].T.astype(bf16)
        out_ref[2 * k, 0] = piece[:BLOCK]
        out_ref[2 * k + 1, 0] = piece[BLOCK:]


def per_device(resid, norm_gain, w_value, d_value, rewards, lengths):
    rolls, slots, width = resid.shape
    rows = rolls * slots
    cols = w_value.shape[1]
    nx, nz, ny, nc = [lax.axis_size(a) for a in DP]
    nzy = nz * ny
    half = width // nc
    chunk = half // nx
    whole = lambda *shape: pl.BlockSpec(shape, lambda *_: (0,) * len(shape))

    near = lax.ppermute(rewards, "y", Y_PAIR)
    w_zy = lax.all_to_all(jnp.broadcast_to(w_value[None], (nzy, BLOCK, cols)), ("zh", "y"), 0, 0, tiled=True)
    w_parts = [w_zy]
    for s in range(1, nx):
        w_parts.append(lax.ppermute(w_zy, "x", X_SHIFTS[s]))
    w_full = jnp.concatenate(w_parts).reshape(half, cols)

    zpart = lax.axis_index("zh")
    place = jnp.stack([lax.axis_index("c"), lax.axis_index("x")]).astype(jnp.int32)
    dval = d_value.reshape(rows, cols)
    rew, near = rewards.reshape(1, rolls), near.reshape(1, rolls)
    step = 32
    own, packed = pl.pallas_call(
        norm_kernel,
        grid=(rows // step,),
        in_specs=[
            pl.BlockSpec(memory_space=pltpu.SMEM),
            pl.BlockSpec((step, width), lambda i: (i, 0)),
            whole(1, width),
            pl.BlockSpec((step, cols), lambda i: (i, 0)),
            whole(1, rolls),
            whole(1, rolls),
            whole(1, rolls),
        ],
        out_specs=[
            pl.BlockSpec((step, half), lambda i: (i, 0)),
            pl.BlockSpec((step, half + 2 * LANES), lambda i: (i, 0)),
        ],
        out_shape=[
            jax.ShapeDtypeStruct((rows, half), bf16),
            jax.ShapeDtypeStruct((rows, half + 2 * LANES), bf16),
        ],
        name="norm_split",
    )(place, resid.reshape(rows, width), norm_gain.reshape(1, width), dval, rew, near, lengths)
    got = lax.ppermute(packed, "c", SWAP)
    send = pl.pallas_call(
        grad_kernel,
        grid_spec=pltpu.PrefetchScalarGridSpec(
            num_scalar_prefetch=1,
            grid=(nx,),
            in_specs=[
                pl.BlockSpec((rows, chunk), lambda k, p: (0, k)),
                pl.BlockSpec((rows, chunk), lambda k, p: (0, k)),
                pl.BlockSpec((rows, cols), lambda k, p: (0, half // LANES)),
                pl.BlockSpec((16, LANES), lambda k, p: (0, half // LANES + 1)),
                whole(rows, cols),
                whole(1, rolls),
                whole(1, rolls),
                whole(1, rolls),
            ],
            out_specs=pl.BlockSpec((1, cols, chunk), lambda k, p: ((p[1] + NX - k) % NX, 0, 0)),
            scratch_shapes=[pltpu.VMEM((rows, cols), bf16), pltpu.VMEM((rows, cols), bf16)],
        ),
        out_shape=jax.ShapeDtypeStruct((nx, cols, chunk), bf16),
        name="grad_partial",
    )(place, own, got, got, got, dval, rew, near, lengths)
    g_x = lax.all_to_all(send, "x", 0, 0, tiled=True)
    g_send = pl.pallas_call(
        turn_kernel,
        grid=(nz,),
        in_specs=[pl.BlockSpec((nx, cols, chunk // nz), lambda k: (0, 0, k))],
        out_specs=pl.BlockSpec((ny, 1, BLOCK, cols), lambda k: (0, k, 0, 0)),
        out_shape=jax.ShapeDtypeStruct((ny, nz, BLOCK, cols), bf16),
        name="sum_turn",
    )(g_x)
    g_y = lax.all_to_all(g_send, "y", 0, 0, tiled=True)
    g_sum = jnp.sum(g_y.astype(f32), axis=0)
    g_z = lax.ppermute(jnp.where(zpart == 0, g_sum[1], g_sum[0]), "zh", SWAP_Z)
    w_grad = (jnp.where(zpart == 0, g_sum[0], g_sum[1]) + g_z).astype(bf16)

    v_other = jnp.dot(got[:, :half], w_full, preferred_element_type=f32)
    v_got = lax.ppermute(v_other, "c", SWAP)
    v_own = jnp.dot(own, w_full, preferred_element_type=f32)
    live = jnp.arange(slots, dtype=jnp.int32)[None, :] < lengths.reshape(rolls, 1)
    value = (v_own + v_got).reshape(rolls, slots, cols) * live.astype(f32)[:, :, None]
    return value.astype(bf16), w_grad


def solution(mesh):
    finer = Mesh(mesh.devices.reshape(4, 2, 8, 2, mesh.shape["tensor"]), DP + ("tensor",))
    placed = (P(DP, None, None), P(), P(DP, "tensor"), P(DP, None, "tensor"), P(DP), P(DP, None))
    return jax.shard_map(
        per_device,
        mesh=finer,
        in_specs=placed,
        out_specs=(P(DP, None, "tensor"), P(DP, "tensor")),
        check_vma=False,
    )
```

```python
import jax
import jax.numpy as jnp
from jax import lax
from jax.experimental import pallas as pl
from jax.experimental.pallas import tpu as pltpu
from jax.sharding import Mesh
from jax.sharding import PartitionSpec as P

DP = ("x", "zh", "y", "c")
SWAP = ((0, 1), (1, 0))
Y_PAIR = tuple((j, j ^ 1) for j in range(8))
LANES = 128
BLOCK = 64
NX = 4
X_SHIFTS = tuple(tuple((j, (j + s) % NX) for j in range(NX)) for s in range(NX))
SWAP_Z = ((0, 1), (1, 0))
bf16, f32 = jnp.bfloat16, jnp.float32


def norm_kernel(core_ref, xpos_ref, x_ref, gain_ref, dval_ref, rew_ref, near_ref, len_ref, own_ref, pack_ref):
    rows, width = x_ref.shape
    total = jnp.zeros((rows, LANES), f32)
    for k in range(width // LANES):
        v = x_ref[:, k * LANES : (k + 1) * LANES].astype(f32)
        total = total + v * v
    scale = lax.rsqrt(jnp.sum(total, axis=1, keepdims=True) * (1.0 / width) + 1e-5)
    first = core_ref[0] == 0
    low = lax.broadcasted_iota(jnp.int32, (rows, LANES), 1) < BLOCK
    tiles = width // LANES // 2
    for k in range(tiles):
        shift, inside = divmod(k, tiles // NX)
        at = (xpos_ref[0] + NX - shift) % NX * (width // NX) + inside * LANES
        next_z = at + width // NX // 2
        at_a, at_b = pl.ds(pl.multiple_of(at, LANES), LANES), pl.ds(pl.multiple_of(next_z, LANES), LANES)
        a = x_ref[:, at_a].astype(f32) * scale * gain_ref[:, at_a]
        b = x_ref[:, at_b].astype(f32) * scale * gain_ref[:, at_b]
        even = jnp.where(low, a, pltpu.roll(b, BLOCK, 1))
        odd = jnp.where(low, pltpu.roll(a, BLOCK, 1), b)
        own_ref[:, k * LANES : (k + 1) * LANES] = jnp.where(first, even, odd).astype(bf16)
        pack_ref[:, k * LANES : (k + 1) * LANES] = jnp.where(first, odd, even).astype(bf16)
    half = width // 2
    pack_ref[:, half : half + LANES] = dval_ref[...]
    lane = lax.broadcasted_iota(jnp.int32, (rows, LANES), 1)
    tail = jnp.zeros((rows, LANES), f32)
    n = rew_ref.shape[1]
    for s, ref in enumerate((rew_ref, near_ref, len_ref)):
        vals = ref[...].astype(f32)
        for j in range(n):
            tail = jnp.where(lane == s * n + j, vals[:, j : j + 1], tail)
    pack_ref[:, half + LANES :] = tail.astype(bf16)


def grad_kernel(xpos_ref, own_ref, got_ref, gotd_ref, tail_ref, dval_ref, rew_ref, near_ref, len_ref, out_ref, ds_own, ds_other):
    rows, _ = dval_ref.shape
    n = rew_ref.shape[1]
    slots = rows // n

    @pl.when(pl.program_id(0) == 0)
    def _():
        rew = rew_ref[...].astype(f32)
        near = near_ref[...].astype(f32)
        tail = tail_ref[...].astype(f32)[0:1, :]
        in_group = lax.broadcasted_iota(jnp.int32, (1, LANES), 1) < 2 * n
        count = 1.0 / (4 * n)
        total = jnp.sum(rew, axis=1, keepdims=True) + jnp.sum(near, axis=1, keepdims=True)
        total = total + jnp.sum(jnp.where(in_group, tail, 0.0), axis=1, keepdims=True)
        mean = total * count
        sq = jnp.sum((rew - mean) ** 2, axis=1, keepdims=True) + jnp.sum((near - mean) ** 2, axis=1, keepdims=True)
        sq = sq + jnp.sum(jnp.where(in_group, (tail - mean) ** 2, 0.0), axis=1, keepdims=True)
        spread = jnp.maximum(jnp.sqrt(sq * count), 0.25)
        row = lax.broadcasted_iota(jnp.int32, (rows, 1), 0)
        place = (row % slots).astype(f32)

        def factor(rewards_at, length_at):
            r = jnp.zeros((rows, 1), f32)
            length = jnp.ones((rows, 1), f32)
            for j in range(n):
                mine = row // slots == j
                r = jnp.where(mine, rewards_at(j), r)
                length = jnp.where(mine, length_at(j), length)
            coef = -((r - mean) / spread) / length
            return jnp.where(place < length, coef, 0.0)

        lens = len_ref[...].astype(f32)
        own = factor(lambda j: rew[:, j : j + 1], lambda j: lens[:, j : j + 1])
        other = factor(lambda j: tail[:, j : j + 1], lambda j: tail[:, 2 * n + j : 2 * n + j + 1])
        ds_own[...] = (dval_ref[...].astype(f32) * own).astype(bf16)
        ds_other[...] = (gotd_ref[...].astype(f32) * other).astype(bf16)

    over_rows = (((0,), (0,)), ((), ()))
    acc = lax.dot_general(ds_own[...], own_ref[...], over_rows, preferred_element_type=f32)
    acc = acc + lax.dot_general(ds_other[...], got_ref[...], over_rows, preferred_element_type=f32)
    for j in range(out_ref.shape[0]):
        out_ref[j] = acc[:, j * LANES : (j + 1) * LANES].astype(bf16)


def per_device(resid, norm_gain, w_value, d_value, rewards, lengths):
    rolls, slots, width = resid.shape
    rows = rolls * slots
    cols = w_value.shape[1]
    nx, nz, ny, nc = [lax.axis_size(a) for a in DP]
    half = width // nc
    chunk = half // nx
    whole = lambda *shape: pl.BlockSpec(shape, lambda *_: (0,) * len(shape))

    near = lax.ppermute(rewards, "y", Y_PAIR)
    w_far = lax.ppermute(w_value, "zh", SWAP_Z)
    zpart = lax.axis_index("zh")
    w_pair = jnp.where(zpart == 0, jnp.stack([w_value, w_far]), jnp.stack([w_far, w_value]))
    w_y = lax.all_to_all(jnp.broadcast_to(w_pair[None], (ny, nz, BLOCK, cols)), "y", 0, 0, tiled=True)
    w_parts = [w_y]
    for s in range(1, nx):
        w_parts.append(lax.ppermute(w_y, "x", X_SHIFTS[s]))
    w_full = jnp.concatenate(w_parts).reshape(half, cols)

    core = lax.axis_index("c").astype(jnp.int32).reshape(1)
    xpos = lax.axis_index("x").astype(jnp.int32).reshape(1)
    dval = d_value.reshape(rows, cols)
    rew, near = rewards.reshape(1, rolls), near.reshape(1, rolls)
    step = 32
    own, packed = pl.pallas_call(
        norm_kernel,
        grid=(rows // step,),
        in_specs=[
            pl.BlockSpec(memory_space=pltpu.SMEM),
            pl.BlockSpec(memory_space=pltpu.SMEM),
            pl.BlockSpec((step, width), lambda i: (i, 0)),
            whole(1, width),
            pl.BlockSpec((step, cols), lambda i: (i, 0)),
            whole(1, rolls),
            whole(1, rolls),
            whole(1, rolls),
        ],
        out_specs=[
            pl.BlockSpec((step, half), lambda i: (i, 0)),
            pl.BlockSpec((step, half + 2 * LANES), lambda i: (i, 0)),
        ],
        out_shape=[
            jax.ShapeDtypeStruct((rows, half), bf16),
            jax.ShapeDtypeStruct((rows, half + 2 * LANES), bf16),
        ],
        name="norm_split",
    )(core, xpos, resid.reshape(rows, width), norm_gain.reshape(1, width), dval, rew, near, lengths)
    got = lax.ppermute(packed, "c", SWAP)
    send = pl.pallas_call(
        grad_kernel,
        grid_spec=pltpu.PrefetchScalarGridSpec(
            num_scalar_prefetch=1,
            grid=(nx,),
            in_specs=[
                pl.BlockSpec((rows, chunk), lambda k, p: (0, k)),
                pl.BlockSpec((rows, chunk), lambda k, p: (0, k)),
                pl.BlockSpec((rows, cols), lambda k, p: (0, half // LANES)),
                pl.BlockSpec((16, LANES), lambda k, p: (0, half // LANES + 1)),
                whole(rows, cols),
                whole(1, rolls),
                whole(1, rolls),
                whole(1, rolls),
            ],
            out_specs=pl.BlockSpec((ny, cols, nz * BLOCK), lambda k, p: ((p[0] + NX - k) % NX, 0, 0)),
            scratch_shapes=[pltpu.VMEM((rows, cols), bf16), pltpu.VMEM((rows, cols), bf16)],
        ),
        out_shape=jax.ShapeDtypeStruct((nx * ny, cols, nz * BLOCK), bf16),
        name="grad_partial",
    )(xpos, own, got, got, got, dval, rew, near, lengths)
    g_xy = lax.all_to_all(send, ("x", "y"), 0, 0, tiled=True)
    g_sum = jnp.sum(g_xy.astype(f32), axis=0).T.reshape(nz, BLOCK, cols)
    g_z = lax.ppermute(jnp.where(zpart == 0, g_sum[1], g_sum[0]), "zh", SWAP_Z)
    w_grad = (jnp.where(zpart == 0, g_sum[0], g_sum[1]) + g_z).astype(bf16)

    v_other = jnp.dot(got[:, :half], w_full, preferred_element_type=f32)
    v_got = lax.ppermute(v_other, "c", SWAP)
    v_own = jnp.dot(own, w_full, preferred_element_type=f32)
    live = jnp.arange(slots, dtype=jnp.int32)[None, :] < lengths.reshape(rolls, 1)
    value = (v_own + v_got).reshape(rolls, slots, cols) * live.astype(f32)[:, :, None]
    return value.astype(bf16), w_grad


def solution(mesh):
    finer = Mesh(mesh.devices.reshape(4, 2, 8, 2, mesh.shape["tensor"]), DP + ("tensor",))
    placed = (P(DP, None, None), P(), P(DP, "tensor"), P(DP, None, "tensor"), P(DP), P(DP, None))
    return jax.shard_map(
        per_device,
        mesh=finer,
        in_specs=placed,
        out_specs=(P(DP, None, "tensor"), P(DP, "tensor")),
        check_vma=False,
    )
```

```python
import jax
import jax.numpy as jnp
from jax import lax
from jax.experimental import pallas as pl
from jax.experimental.pallas import tpu as pltpu
from jax.sharding import Mesh
from jax.sharding import PartitionSpec as P

DP = ("x", "zh", "y", "c")
SWAP = ((0, 1), (1, 0))
Y_PAIR = tuple((j, j ^ 1) for j in range(8))
LANES = 128
BLOCK = 64
NX = 4
X_SHIFTS = tuple(tuple((j, (j + s) % NX) for j in range(NX)) for s in range(NX))
SWAP_Z = ((0, 1), (1, 0))
bf16, f32 = jnp.bfloat16, jnp.float32


def norm_kernel(core_ref, xpos_ref, x_ref, gain_ref, dval_ref, rew_ref, near_ref, len_ref, own_ref, pack_ref):
    rows, width = x_ref.shape
    total = jnp.zeros((rows, LANES), f32)
    for k in range(width // LANES):
        v = x_ref[:, k * LANES : (k + 1) * LANES].astype(f32)
        total = total + v * v
    scale = lax.rsqrt(jnp.sum(total, axis=1, keepdims=True) * (1.0 / width) + 1e-5)
    first = core_ref[0] == 0
    low = lax.broadcasted_iota(jnp.int32, (rows, LANES), 1) < BLOCK
    tiles = width // LANES // 2
    for k in range(tiles):
        shift, inside = divmod(k, tiles // NX)
        at = (xpos_ref[0] + NX - shift) % NX * (width // NX) + inside * LANES
        next_z = at + width // NX // 2
        at_a, at_b = pl.ds(pl.multiple_of(at, LANES), LANES), pl.ds(pl.multiple_of(next_z, LANES), LANES)
        a = x_ref[:, at_a].astype(f32) * scale * gain_ref[:, at_a]
        b = x_ref[:, at_b].astype(f32) * scale * gain_ref[:, at_b]
        even = jnp.where(low, a, pltpu.roll(b, BLOCK, 1))
        odd = jnp.where(low, pltpu.roll(a, BLOCK, 1), b)
        own_ref[:, k * LANES : (k + 1) * LANES] = jnp.where(first, even, odd).astype(bf16)
        pack_ref[:, k * LANES : (k + 1) * LANES] = jnp.where(first, odd, even).astype(bf16)
    half = width // 2
    pack_ref[:, half : half + LANES] = dval_ref[...]
    lane = lax.broadcasted_iota(jnp.int32, (rows, LANES), 1)
    tail = jnp.zeros((rows, LANES), f32)
    n = rew_ref.shape[1]
    for s, ref in enumerate((rew_ref, near_ref, len_ref)):
        vals = ref[...].astype(f32)
        for j in range(n):
            tail = jnp.where(lane == s * n + j, vals[:, j : j + 1], tail)
    pack_ref[:, half + LANES :] = tail.astype(bf16)


def grad_kernel(xpos_ref, own_ref, got_ref, gotd_ref, tail_ref, dval_ref, rew_ref, near_ref, len_ref, out_ref, ds_own, ds_other):
    rows, _ = dval_ref.shape
    n = rew_ref.shape[1]
    slots = rows // n

    @pl.when(pl.program_id(0) == 0)
    def _():
        rew = rew_ref[...].astype(f32)
        near = near_ref[...].astype(f32)
        tail = tail_ref[...].astype(f32)[0:1, :]
        in_group = lax.broadcasted_iota(jnp.int32, (1, LANES), 1) < 2 * n
        count = 1.0 / (4 * n)
        total = jnp.sum(rew, axis=1, keepdims=True) + jnp.sum(near, axis=1, keepdims=True)
        total = total + jnp.sum(jnp.where(in_group, tail, 0.0), axis=1, keepdims=True)
        mean = total * count
        sq = jnp.sum((rew - mean) ** 2, axis=1, keepdims=True) + jnp.sum((near - mean) ** 2, axis=1, keepdims=True)
        sq = sq + jnp.sum(jnp.where(in_group, (tail - mean) ** 2, 0.0), axis=1, keepdims=True)
        spread = jnp.maximum(jnp.sqrt(sq * count), 0.25)
        row = lax.broadcasted_iota(jnp.int32, (rows, 1), 0)
        place = (row % slots).astype(f32)

        def factor(rewards_at, length_at):
            r = jnp.zeros((rows, 1), f32)
            length = jnp.ones((rows, 1), f32)
            for j in range(n):
                mine = row // slots == j
                r = jnp.where(mine, rewards_at(j), r)
                length = jnp.where(mine, length_at(j), length)
            coef = -((r - mean) / spread) / length
            return jnp.where(place < length, coef, 0.0)

        lens = len_ref[...].astype(f32)
        own = factor(lambda j: rew[:, j : j + 1], lambda j: lens[:, j : j + 1])
        other = factor(lambda j: tail[:, j : j + 1], lambda j: tail[:, 2 * n + j : 2 * n + j + 1])
        ds_own[...] = (dval_ref[...].astype(f32) * own).astype(bf16)
        ds_other[...] = (gotd_ref[...].astype(f32) * other).astype(bf16)

    over_rows = (((0,), (0,)), ((), ()))
    acc = lax.dot_general(ds_own[...], own_ref[...], over_rows, preferred_element_type=f32)
    acc = acc + lax.dot_general(ds_other[...], got_ref[...], over_rows, preferred_element_type=f32)
    for j in range(out_ref.shape[0]):
        out_ref[j] = acc[:, j * LANES : (j + 1) * LANES].astype(bf16)


def per_device(resid, norm_gain, w_value, d_value, rewards, lengths):
    rolls, slots, width = resid.shape
    rows = rolls * slots
    cols = w_value.shape[1]
    nx, nz, ny, nc = [lax.axis_size(a) for a in DP]
    half = width // nc
    chunk = half // nx
    whole = lambda *shape: pl.BlockSpec(shape, lambda *_: (0,) * len(shape))

    near = lax.ppermute(rewards, "y", Y_PAIR)
    w_y = lax.all_to_all(jnp.broadcast_to(w_value[None], (ny, BLOCK, cols)), "y", 0, 0, tiled=True)
    w_far = lax.ppermute(w_y, "zh", SWAP_Z)
    zpart = lax.axis_index("zh")
    w_pair = jnp.where(zpart == 0, jnp.stack([w_y, w_far], axis=1), jnp.stack([w_far, w_y], axis=1))
    w_parts = [w_pair]
    for s in range(1, nx):
        w_parts.append(lax.ppermute(w_pair, "x", X_SHIFTS[s]))
    w_full = jnp.concatenate(w_parts).reshape(half, cols)

    core = lax.axis_index("c").astype(jnp.int32).reshape(1)
    xpos = lax.axis_index("x").astype(jnp.int32).reshape(1)
    dval = d_value.reshape(rows, cols)
    rew, near = rewards.reshape(1, rolls), near.reshape(1, rolls)
    step = 32
    own, packed = pl.pallas_call(
        norm_kernel,
        grid=(rows // step,),
        in_specs=[
            pl.BlockSpec(memory_space=pltpu.SMEM),
            pl.BlockSpec(memory_space=pltpu.SMEM),
            pl.BlockSpec((step, width), lambda i: (i, 0)),
            whole(1, width),
            pl.BlockSpec((step, cols), lambda i: (i, 0)),
            whole(1, rolls),
            whole(1, rolls),
            whole(1, rolls),
        ],
        out_specs=[
            pl.BlockSpec((step, half), lambda i: (i, 0)),
            pl.BlockSpec((step, half + 2 * LANES), lambda i: (i, 0)),
        ],
        out_shape=[
            jax.ShapeDtypeStruct((rows, half), bf16),
            jax.ShapeDtypeStruct((rows, half + 2 * LANES), bf16),
        ],
        name="norm_split",
    )(core, xpos, resid.reshape(rows, width), norm_gain.reshape(1, width), dval, rew, near, lengths)
    got = lax.ppermute(packed, "c", SWAP)
    send = pl.pallas_call(
        grad_kernel,
        grid_spec=pltpu.PrefetchScalarGridSpec(
            num_scalar_prefetch=1,
            grid=(nx,),
            in_specs=[
                pl.BlockSpec((rows, chunk), lambda k, p: (0, k)),
                pl.BlockSpec((rows, chunk), lambda k, p: (0, k)),
                pl.BlockSpec((rows, cols), lambda k, p: (0, half // LANES)),
                pl.BlockSpec((16, LANES), lambda k, p: (0, half // LANES + 1)),
                whole(rows, cols),
                whole(1, rolls),
                whole(1, rolls),
                whole(1, rolls),
            ],
            out_specs=pl.BlockSpec((ny, cols, nz * BLOCK), lambda k, p: ((p[0] + NX - k) % NX, 0, 0)),
            scratch_shapes=[pltpu.VMEM((rows, cols), bf16), pltpu.VMEM((rows, cols), bf16)],
        ),
        out_shape=jax.ShapeDtypeStruct((nx * ny, cols, nz * BLOCK), bf16),
        name="grad_partial",
    )(xpos, own, got, got, got, dval, rew, near, lengths)
    g_xy = lax.all_to_all(send, ("x", "y"), 0, 0, tiled=True)
    g_sum = jnp.sum(g_xy.astype(f32), axis=0).T.reshape(nz, BLOCK, cols)
    g_z = lax.ppermute(jnp.where(zpart == 0, g_sum[1], g_sum[0]), "zh", SWAP_Z)
    w_grad = (jnp.where(zpart == 0, g_sum[0], g_sum[1]) + g_z).astype(bf16)

    v_other = jnp.dot(got[:, :half], w_full, preferred_element_type=f32)
    v_got = lax.ppermute(v_other, "c", SWAP)
    v_own = jnp.dot(own, w_full, preferred_element_type=f32)
    live = jnp.arange(slots, dtype=jnp.int32)[None, :] < lengths.reshape(rolls, 1)
    value = (v_own + v_got).reshape(rolls, slots, cols) * live.astype(f32)[:, :, None]
    return value.astype(bf16), w_grad


def solution(mesh):
    finer = Mesh(mesh.devices.reshape(4, 2, 8, 2, mesh.shape["tensor"]), DP + ("tensor",))
    placed = (P(DP, None, None), P(), P(DP, "tensor"), P(DP, None, "tensor"), P(DP), P(DP, None))
    return jax.shard_map(
        per_device,
        mesh=finer,
        in_specs=placed,
        out_specs=(P(DP, None, "tensor"), P(DP, "tensor")),
        check_vma=False,
    )
```

```python
import jax
import jax.numpy as jnp
from jax import lax
from jax.experimental import pallas as pl
from jax.experimental.pallas import tpu as pltpu
from jax.sharding import Mesh
from jax.sharding import PartitionSpec as P

DP = ("x", "zh", "y", "c")
SWAP = ((0, 1), (1, 0))
Y_PAIR = tuple((j, j ^ 1) for j in range(8))
LANES = 128
BLOCK = 64
NX = 4
X_SHIFTS = tuple(tuple((j, (j + s) % NX) for j in range(NX)) for s in range(NX))
SWAP_Z = ((0, 1), (1, 0))
bf16, f32 = jnp.bfloat16, jnp.float32


def norm_kernel(core_ref, xpos_ref, x_ref, gain_ref, dval_ref, rew_ref, near_ref, len_ref, own_ref, pack_ref):
    rows, width = x_ref.shape
    total = jnp.zeros((rows, LANES), f32)
    for k in range(width // LANES):
        v = x_ref[:, k * LANES : (k + 1) * LANES].astype(f32)
        total = total + v * v
    scale = lax.rsqrt(jnp.sum(total, axis=1, keepdims=True) * (1.0 / width) + 1e-5)
    first = core_ref[0] == 0
    here = pl.ds(pl.multiple_of(pl.program_id(0) * rows, rows), rows)
    low = lax.broadcasted_iota(jnp.int32, (rows, LANES), 1) < BLOCK
    tiles = width // LANES // 2
    for k in range(tiles):
        shift, inside = divmod(k, tiles // NX)
        at = (xpos_ref[0] + NX - shift) % NX * (width // NX) + inside * LANES
        next_z = at + width // NX // 2
        at_a, at_b = pl.ds(pl.multiple_of(at, LANES), LANES), pl.ds(pl.multiple_of(next_z, LANES), LANES)
        a = x_ref[:, at_a].astype(f32) * scale * gain_ref[:, at_a]
        b = x_ref[:, at_b].astype(f32) * scale * gain_ref[:, at_b]
        crossed = pltpu.roll(jnp.where(low, b, a), BLOCK, 1)
        even = jnp.where(low, a, crossed)
        odd = jnp.where(low, crossed, b)
        own_ref[here, k * LANES : (k + 1) * LANES] = jnp.where(first, even, odd).astype(bf16)
        pack_ref[here, k * LANES : (k + 1) * LANES] = jnp.where(first, odd, even).astype(bf16)
    half = width // 2
    pack_ref[here, half : half + LANES] = dval_ref[...]
    lane = lax.broadcasted_iota(jnp.int32, (rows, LANES), 1)
    tail = jnp.zeros((rows, LANES), f32)
    n = rew_ref.shape[1]
    for s, ref in enumerate((rew_ref, near_ref, len_ref)):
        vals = ref[...].astype(f32)
        for j in range(n):
            tail = jnp.where(lane == s * n + j, vals[:, j : j + 1], tail)
    pack_ref[here, half + LANES :] = tail.astype(bf16)


def grad_kernel(xpos_ref, own_ref, got_ref, dval_ref, rew_ref, near_ref, len_ref, out_ref, ds_own, ds_other):
    rows, cols = dval_ref.shape
    half = own_ref.shape[1]
    chunk = half // NX
    n = rew_ref.shape[1]
    slots = rows // n

    @pl.when(pl.program_id(0) == 0)
    def _():
        rew = rew_ref[...].astype(f32)
        near = near_ref[...].astype(f32)
        tail = got_ref[:16, half + cols :].astype(f32)[0:1, :]
        in_group = lax.broadcasted_iota(jnp.int32, (1, LANES), 1) < 2 * n
        count = 1.0 / (4 * n)
        total = jnp.sum(rew, axis=1, keepdims=True) + jnp.sum(near, axis=1, keepdims=True)
        total = total + jnp.sum(jnp.where(in_group, tail, 0.0), axis=1, keepdims=True)
        mean = total * count
        sq = jnp.sum((rew - mean) ** 2, axis=1, keepdims=True) + jnp.sum((near - mean) ** 2, axis=1, keepdims=True)
        sq = sq + jnp.sum(jnp.where(in_group, (tail - mean) ** 2, 0.0), axis=1, keepdims=True)
        spread = jnp.maximum(jnp.sqrt(sq * count), 0.25)
        row = lax.broadcasted_iota(jnp.int32, (rows, 1), 0)
        place = (row % slots).astype(f32)

        def factor(rewards_at, length_at):
            r = jnp.zeros((rows, 1), f32)
            length = jnp.ones((rows, 1), f32)
            for j in range(n):
                mine = row // slots == j
                r = jnp.where(mine, rewards_at(j), r)
                length = jnp.where(mine, length_at(j), length)
            coef = -((r - mean) / spread) / length
            return jnp.where(place < length, coef, 0.0)

        lens = len_ref[...].astype(f32)
        own = factor(lambda j: rew[:, j : j + 1], lambda j: lens[:, j : j + 1])
        other = factor(lambda j: tail[:, j : j + 1], lambda j: tail[:, 2 * n + j : 2 * n + j + 1])
        ds_own[...] = (dval_ref[...].astype(f32) * own).T.astype(bf16)
        ds_other[...] = (got_ref[:, half : half + cols].astype(f32) * other).T.astype(bf16)

    here = pl.ds(pl.multiple_of(pl.program_id(0) * chunk, chunk), chunk)
    acc = jnp.dot(ds_own[...], own_ref[:, here], preferred_element_type=f32)
    acc = acc + jnp.dot(ds_other[...], got_ref[:, here], preferred_element_type=f32)
    for j in range(out_ref.shape[0]):
        out_ref[j] = acc[:, j * LANES : (j + 1) * LANES].astype(bf16)


def on_chip(array):
    return pltpu.with_memory_space_constraint(array, pltpu.VMEM)


def per_device(resid, norm_gain, w_value, d_value, rewards, lengths):
    rolls, slots, width = resid.shape
    rows = rolls * slots
    cols = w_value.shape[1]
    nx, nz, ny, nc = [lax.axis_size(a) for a in DP]
    half = width // nc
    whole = lambda *shape: pl.BlockSpec(shape, lambda *_: (0,) * len(shape))

    near = lax.ppermute(rewards, "y", Y_PAIR)
    w_y = lax.all_to_all(jnp.broadcast_to(w_value[None], (ny, BLOCK, cols)), "y", 0, 0, tiled=True)
    w_far = lax.ppermute(w_y, "zh", SWAP_Z)
    zpart = lax.axis_index("zh")
    w_pair = jnp.where(zpart == 0, jnp.stack([w_y, w_far], axis=1), jnp.stack([w_far, w_y], axis=1))
    w_parts = [w_pair]
    for s in range(1, nx):
        w_parts.append(lax.ppermute(w_pair, "x", X_SHIFTS[s]))
    w_full = jnp.concatenate(w_parts).reshape(half, cols)

    core = lax.axis_index("c").astype(jnp.int32).reshape(1)
    xpos = lax.axis_index("x").astype(jnp.int32).reshape(1)
    dval = d_value.reshape(rows, cols)
    rew, near = rewards.reshape(1, rolls), on_chip(near.reshape(1, rolls))
    step = 64
    own, packed = pl.pallas_call(
        norm_kernel,
        grid=(rows // step,),
        in_specs=[
            pl.BlockSpec(memory_space=pltpu.SMEM),
            pl.BlockSpec(memory_space=pltpu.SMEM),
            pl.BlockSpec((step, width), lambda i: (i, 0)),
            whole(1, width),
            pl.BlockSpec((step, cols), lambda i: (i, 0)),
            whole(1, rolls),
            pl.BlockSpec(memory_space=pltpu.VMEM),
            whole(1, rolls),
        ],
        out_specs=[pl.BlockSpec(memory_space=pltpu.VMEM), pl.BlockSpec(memory_space=pltpu.VMEM)],
        out_shape=[pltpu.VMEM((rows, half), bf16), pltpu.VMEM((rows, half + 2 * LANES), bf16)],
        name="norm_split",
    )(core, xpos, resid.reshape(rows, width), norm_gain.reshape(1, width), dval, rew, near, lengths)
    got = lax.ppermute(packed, "c", SWAP)
    got_in, own_in = on_chip(got), on_chip(own)
    send = pl.pallas_call(
        grad_kernel,
        grid_spec=pltpu.PrefetchScalarGridSpec(
            num_scalar_prefetch=1,
            grid=(nx,),
            in_specs=[
                pl.BlockSpec(memory_space=pltpu.VMEM),
                pl.BlockSpec(memory_space=pltpu.VMEM),
                whole(rows, cols),
                whole(1, rolls),
                pl.BlockSpec(memory_space=pltpu.VMEM),
                whole(1, rolls),
            ],
            out_specs=pl.BlockSpec((ny, cols, nz * BLOCK), lambda k, p: ((p[0] + NX - k) % NX, 0, 0)),
            scratch_shapes=[pltpu.VMEM((cols, rows), bf16), pltpu.VMEM((cols, rows), bf16)],
        ),
        out_shape=jax.ShapeDtypeStruct((nx * ny, cols, nz * BLOCK), bf16),
        name="grad_partial",
    )(xpos, own_in, got_in, dval, rew, near, lengths)
    g_xy = lax.all_to_all(send, ("x", "y"), 0, 0, tiled=True)
    g_sum = jnp.sum(g_xy.astype(f32), axis=0).T.reshape(nz, BLOCK, cols)
    g_z = lax.ppermute(jnp.where(zpart == 0, g_sum[1], g_sum[0]), "zh", SWAP_Z)
    w_grad = (jnp.where(zpart == 0, g_sum[0], g_sum[1]) + g_z).astype(bf16)

    v_other = jnp.dot(got[:, :half], w_full, preferred_element_type=f32)
    v_got = lax.ppermute(v_other, "c", SWAP)
    v_own = jnp.dot(own, w_full, preferred_element_type=f32)
    live = jnp.arange(slots, dtype=jnp.int32)[None, :] < lengths.reshape(rolls, 1)
    value = (v_own + v_got).reshape(rolls, slots, cols) * live.astype(f32)[:, :, None]
    value = value.astype(bf16)
    return value, w_grad


def solution(mesh):
    finer = Mesh(mesh.devices.reshape(4, 2, 8, 2, mesh.shape["tensor"]), DP + ("tensor",))
    placed = (P(DP, None, None), P(), P(DP, "tensor"), P(DP, None, "tensor"), P(DP), P(DP, None))
    return jax.shard_map(
        per_device,
        mesh=finer,
        in_specs=placed,
        out_specs=(P(DP, None, "tensor"), P(DP, "tensor")),
        check_vma=False,
    )
```

```python
import jax
import jax.numpy as jnp
from jax import lax
from jax.experimental import pallas as pl
from jax.experimental.pallas import tpu as pltpu
from jax.sharding import Mesh
from jax.sharding import PartitionSpec as P

DP = ("x", "zh", "y", "c")
SWAP = ((0, 1), (1, 0))
Y_PAIR = tuple((j, j ^ 1) for j in range(8))
LANES = 128
BLOCK = 64
VMEM_GRANT = 10 * 2**20
NX = 4
X_SHIFTS = tuple(tuple((j, (j + s) % NX) for j in range(NX)) for s in range(NX))
SWAP_Z = ((0, 1), (1, 0))
bf16, f32 = jnp.bfloat16, jnp.float32


def norm_kernel(core_ref, xpos_ref, x_ref, gain_ref, dval_ref, rew_ref, near_ref, len_ref, own_ref, pack_ref):
    rows, width = x_ref.shape
    total = jnp.zeros((rows, LANES), f32)
    for k in range(width // LANES):
        v = x_ref[:, k * LANES : (k + 1) * LANES].astype(f32)
        total = total + v * v
    scale = lax.rsqrt(jnp.sum(total, axis=1, keepdims=True) * (1.0 / width) + 1e-5)
    first = core_ref[0] == 0
    here = pl.ds(pl.multiple_of(pl.program_id(0) * rows, rows), rows)
    low = lax.broadcasted_iota(jnp.int32, (rows, LANES), 1) < BLOCK
    tiles = width // LANES // 2
    for k in range(tiles):
        shift, inside = divmod(k, tiles // NX)
        at = (xpos_ref[0] + NX - shift) % NX * (width // NX) + inside * LANES
        next_z = at + width // NX // 2
        at_a, at_b = pl.ds(pl.multiple_of(at, LANES), LANES), pl.ds(pl.multiple_of(next_z, LANES), LANES)
        a = x_ref[:, at_a].astype(f32) * scale * gain_ref[:, at_a]
        b = x_ref[:, at_b].astype(f32) * scale * gain_ref[:, at_b]
        crossed = pltpu.roll(jnp.where(low, b, a), BLOCK, 1)
        even = jnp.where(low, a, crossed)
        odd = jnp.where(low, crossed, b)
        own_ref[here, k * LANES : (k + 1) * LANES] = jnp.where(first, even, odd).astype(bf16)
        pack_ref[here, k * LANES : (k + 1) * LANES] = jnp.where(first, odd, even).astype(bf16)
    half = width // 2
    pack_ref[here, half : half + LANES] = dval_ref[...]
    lane = lax.broadcasted_iota(jnp.int32, (rows, LANES), 1)
    tail = jnp.zeros((rows, LANES), f32)
    n = rew_ref.shape[1]
    for s, ref in enumerate((rew_ref, near_ref, len_ref)):
        vals = ref[...].astype(f32)
        for j in range(n):
            tail = jnp.where(lane == s * n + j, vals[:, j : j + 1], tail)
    pack_ref[here, half + LANES :] = tail.astype(bf16)


def grad_kernel(xpos_ref, own_ref, got_ref, dval_ref, rew_ref, near_ref, len_ref, out_ref, ds_own, ds_other):
    rows, cols = dval_ref.shape
    half = own_ref.shape[1]
    chunk = half // NX
    n = rew_ref.shape[1]
    slots = rows // n

    @pl.when(pl.program_id(0) == 0)
    def _():
        rew = rew_ref[...].astype(f32)
        near = near_ref[...].astype(f32)
        tail = got_ref[:16, half + cols :].astype(f32)[0:1, :]
        in_group = lax.broadcasted_iota(jnp.int32, (1, LANES), 1) < 2 * n
        count = 1.0 / (4 * n)
        total = jnp.sum(rew, axis=1, keepdims=True) + jnp.sum(near, axis=1, keepdims=True)
        total = total + jnp.sum(jnp.where(in_group, tail, 0.0), axis=1, keepdims=True)
        mean = total * count
        sq = jnp.sum((rew - mean) ** 2, axis=1, keepdims=True) + jnp.sum((near - mean) ** 2, axis=1, keepdims=True)
        sq = sq + jnp.sum(jnp.where(in_group, (tail - mean) ** 2, 0.0), axis=1, keepdims=True)
        spread = jnp.maximum(jnp.sqrt(sq * count), 0.25)
        row = lax.broadcasted_iota(jnp.int32, (rows, 1), 0)
        place = (row % slots).astype(f32)

        def factor(rewards_at, length_at):
            r = jnp.zeros((rows, 1), f32)
            length = jnp.ones((rows, 1), f32)
            for j in range(n):
                mine = row // slots == j
                r = jnp.where(mine, rewards_at(j), r)
                length = jnp.where(mine, length_at(j), length)
            coef = -((r - mean) / spread) / length
            return jnp.where(place < length, coef, 0.0)

        lens = len_ref[...].astype(f32)
        own = factor(lambda j: rew[:, j : j + 1], lambda j: lens[:, j : j + 1])
        other = factor(lambda j: tail[:, j : j + 1], lambda j: tail[:, 2 * n + j : 2 * n + j + 1])
        ds_own[...] = (dval_ref[...].astype(f32) * own).T.astype(bf16)
        ds_other[...] = (got_ref[:, half : half + cols].astype(f32) * other).T.astype(bf16)

    here = pl.ds(pl.multiple_of(pl.program_id(0) * chunk, chunk), chunk)
    acc = jnp.dot(ds_own[...], own_ref[:, here], preferred_element_type=f32)
    acc = acc + jnp.dot(ds_other[...], got_ref[:, here], preferred_element_type=f32)
    for j in range(out_ref.shape[0]):
        out_ref[j] = acc[:, j * LANES : (j + 1) * LANES].astype(bf16)


def value_kernel(z_ref, got_ref, own_ref, *refs):
    *parts, v_other_ref, v_own_ref, w_ref = refs
    first = z_ref[0] == 0
    for s, (near, far) in enumerate(zip(parts[:NX], parts[NX:])):
        for y in range(near.shape[0]):
            at = (s * near.shape[0] + y) * 2 * BLOCK
            a, b = near[y].astype(f32), far[y].astype(f32)
            w_ref[at : at + BLOCK] = jnp.where(first, a, b).astype(bf16)
            w_ref[at + BLOCK : at + 2 * BLOCK] = jnp.where(first, b, a).astype(bf16)
    half = w_ref.shape[0]
    v_other_ref[...] = jnp.dot(got_ref[:, :half], w_ref[...], preferred_element_type=f32)
    v_own_ref[...] = jnp.dot(own_ref[...], w_ref[...], preferred_element_type=f32)


def on_chip(array):
    return pltpu.with_memory_space_constraint(array, pltpu.VMEM)


def per_device(resid, norm_gain, w_value, d_value, rewards, lengths):
    rolls, slots, width = resid.shape
    rows = rolls * slots
    cols = w_value.shape[1]
    nx, nz, ny, nc = [lax.axis_size(a) for a in DP]
    half = width // nc
    whole = lambda *shape: pl.BlockSpec(shape, lambda *_: (0,) * len(shape))

    near = lax.ppermute(rewards, "y", Y_PAIR)
    w_y = lax.all_to_all(jnp.broadcast_to(w_value[None], (ny, BLOCK, cols)), "y", 0, 0, tiled=True)
    w_far = lax.ppermute(w_y, "zh", SWAP_Z)
    zpart = lax.axis_index("zh")
    own_w, far_w = [w_y], [w_far]
    for s in range(1, nx):
        own_w.append(lax.ppermute(w_y, "x", X_SHIFTS[s]))
        far_w.append(lax.ppermute(w_far, "x", X_SHIFTS[s]))
    core = lax.axis_index("c").astype(jnp.int32).reshape(1)
    xpos = lax.axis_index("x").astype(jnp.int32).reshape(1)
    zpos = zpart.astype(jnp.int32).reshape(1)
    dval = d_value.reshape(rows, cols)
    rew, near = rewards.reshape(1, rolls), on_chip(near.reshape(1, rolls))
    step = 64
    own, packed = pl.pallas_call(
        norm_kernel,
        grid=(rows // step,),
        in_specs=[
            pl.BlockSpec(memory_space=pltpu.SMEM),
            pl.BlockSpec(memory_space=pltpu.SMEM),
            pl.BlockSpec((step, width), lambda i: (i, 0)),
            whole(1, width),
            pl.BlockSpec((step, cols), lambda i: (i, 0)),
            whole(1, rolls),
            pl.BlockSpec(memory_space=pltpu.VMEM),
            whole(1, rolls),
        ],
        out_specs=[pl.BlockSpec(memory_space=pltpu.VMEM), pl.BlockSpec(memory_space=pltpu.VMEM)],
        out_shape=[pltpu.VMEM((rows, half), bf16), pltpu.VMEM((rows, half + 2 * LANES), bf16)],
        name="norm_split",
    )(core, xpos, resid.reshape(rows, width), norm_gain.reshape(1, width), dval, rew, near, lengths)
    got = lax.ppermute(packed, "c", SWAP)
    got_in, own_in = on_chip(got), on_chip(own)
    send = pl.pallas_call(
        grad_kernel,
        grid_spec=pltpu.PrefetchScalarGridSpec(
            num_scalar_prefetch=1,
            grid=(nx,),
            in_specs=[
                pl.BlockSpec(memory_space=pltpu.VMEM),
                pl.BlockSpec(memory_space=pltpu.VMEM),
                whole(rows, cols),
                whole(1, rolls),
                pl.BlockSpec(memory_space=pltpu.VMEM),
                whole(1, rolls),
            ],
            out_specs=pl.BlockSpec((ny, cols, nz * BLOCK), lambda k, p: ((p[0] + NX - k) % NX, 0, 0)),
            scratch_shapes=[pltpu.VMEM((cols, rows), bf16), pltpu.VMEM((cols, rows), bf16)],
        ),
        out_shape=jax.ShapeDtypeStruct((nx * ny, cols, nz * BLOCK), bf16),
        compiler_params=pltpu.CompilerParams(vmem_limit_bytes=VMEM_GRANT),
        name="grad_partial",
    )(xpos, own_in, got_in, dval, rew, near, lengths)
    g_xy = lax.all_to_all(send, ("x", "y"), 0, 0, tiled=True)
    g_sum = jnp.sum(g_xy.astype(f32), axis=0).T.reshape(nz, BLOCK, cols)
    g_z = lax.ppermute(jnp.where(zpart == 0, g_sum[1], g_sum[0]), "zh", SWAP_Z)
    w_grad = (jnp.where(zpart == 0, g_sum[0], g_sum[1]) + g_z).astype(bf16)

    in_vmem = pl.BlockSpec(memory_space=pltpu.VMEM)
    v_other, v_own = pl.pallas_call(
        value_kernel,
        in_specs=[pl.BlockSpec(memory_space=pltpu.SMEM)] + [in_vmem] * (2 + 2 * nx),
        out_specs=[in_vmem, in_vmem],
        out_shape=[pltpu.VMEM((rows, cols), f32), pltpu.VMEM((rows, cols), f32)],
        scratch_shapes=[pltpu.VMEM((half, cols), bf16)],
        compiler_params=pltpu.CompilerParams(vmem_limit_bytes=VMEM_GRANT),
        name="value_parts",
    )(zpos, got_in, own_in, *[on_chip(w) for w in own_w + far_w])
    v_got = lax.ppermute(v_other, "c", SWAP)
    live = jnp.arange(slots, dtype=jnp.int32)[None, :] < lengths.reshape(rolls, 1)
    value = (v_own + v_got).reshape(rolls, slots, cols) * live.astype(f32)[:, :, None]
    value = value.astype(bf16)
    return value, w_grad


def solution(mesh):
    finer = Mesh(mesh.devices.reshape(4, 2, 8, 2, mesh.shape["tensor"]), DP + ("tensor",))
    placed = (P(DP, None, None), P(), P(DP, "tensor"), P(DP, None, "tensor"), P(DP), P(DP, None))
    return jax.shard_map(
        per_device,
        mesh=finer,
        in_specs=placed,
        out_specs=(P(DP, None, "tensor"), P(DP, "tensor")),
        check_vma=False,
    )
```

```python
import jax
import jax.numpy as jnp
from jax import lax
from jax.experimental import pallas as pl
from jax.experimental.pallas import tpu as pltpu
from jax.sharding import Mesh
from jax.sharding import PartitionSpec as P

DP = ("x", "zh", "y", "c")
SWAP = ((0, 1), (1, 0))
Y_PAIR = tuple((j, j ^ 1) for j in range(8))
LANES = 128
BLOCK = 64
VMEM_GRANT = 10 * 2**20
NX = 4
X_SHIFTS = tuple(tuple((j, (j + s) % NX) for j in range(NX)) for s in range(NX))
SWAP_Z = ((0, 1), (1, 0))
bf16, f32 = jnp.bfloat16, jnp.float32


def norm_kernel(core_ref, xpos_ref, x_ref, gain_ref, dval_ref, rew_ref, near_ref, len_ref, own_ref, pack_ref):
    rows, width = x_ref.shape
    total = jnp.zeros((rows, LANES), f32)
    for k in range(width // LANES):
        v = x_ref[:, k * LANES : (k + 1) * LANES].astype(f32)
        total = total + v * v
    scale = lax.rsqrt(jnp.sum(total, axis=1, keepdims=True) * (1.0 / width) + 1e-5)
    first = core_ref[0] == 0
    here = pl.ds(pl.multiple_of(pl.program_id(0) * rows, rows), rows)
    low = lax.broadcasted_iota(jnp.int32, (rows, LANES), 1) < BLOCK
    tiles = width // LANES // 2
    for k in range(tiles):
        shift, inside = divmod(k, tiles // NX)
        at = (xpos_ref[0] + NX - shift) % NX * (width // NX) + inside * LANES
        next_z = at + width // NX // 2
        at_a, at_b = pl.ds(pl.multiple_of(at, LANES), LANES), pl.ds(pl.multiple_of(next_z, LANES), LANES)
        a = x_ref[:, at_a].astype(f32) * scale * gain_ref[:, at_a]
        b = x_ref[:, at_b].astype(f32) * scale * gain_ref[:, at_b]
        crossed = pltpu.roll(jnp.where(low, b, a), BLOCK, 1)
        even = jnp.where(low, a, crossed)
        odd = jnp.where(low, crossed, b)
        own_ref[here, k * LANES : (k + 1) * LANES] = jnp.where(first, even, odd).astype(bf16)
        pack_ref[here, k * LANES : (k + 1) * LANES] = jnp.where(first, odd, even).astype(bf16)
    half = width // 2
    pack_ref[here, half : half + LANES] = dval_ref[...]
    lane = lax.broadcasted_iota(jnp.int32, (rows, LANES), 1)
    tail = jnp.zeros((rows, LANES), f32)
    n = rew_ref.shape[1]
    for s, ref in enumerate((rew_ref, near_ref, len_ref)):
        vals = ref[...].astype(f32)
        for j in range(n):
            tail = jnp.where(lane == s * n + j, vals[:, j : j + 1], tail)
    pack_ref[here, half + LANES :] = tail.astype(bf16)


def grad_kernel(xpos_ref, own_ref, got_ref, dval_ref, rew_ref, near_ref, len_ref, out_ref, ds_own, ds_other):
    rows, cols = dval_ref.shape
    half = own_ref.shape[1]
    chunk = half // NX
    n = rew_ref.shape[1]
    slots = rows // n

    @pl.when(pl.program_id(0) == 0)
    def _():
        rew = rew_ref[...].astype(f32)
        near = near_ref[...].astype(f32)
        tail = got_ref[:16, half + cols :].astype(f32)[0:1, :]
        in_group = lax.broadcasted_iota(jnp.int32, (1, LANES), 1) < 2 * n
        count = 1.0 / (4 * n)
        total = jnp.sum(rew, axis=1, keepdims=True) + jnp.sum(near, axis=1, keepdims=True)
        total = total + jnp.sum(jnp.where(in_group, tail, 0.0), axis=1, keepdims=True)
        mean = total * count
        sq = jnp.sum((rew - mean) ** 2, axis=1, keepdims=True) + jnp.sum((near - mean) ** 2, axis=1, keepdims=True)
        sq = sq + jnp.sum(jnp.where(in_group, (tail - mean) ** 2, 0.0), axis=1, keepdims=True)
        spread = jnp.maximum(jnp.sqrt(sq * count), 0.25)
        row = lax.broadcasted_iota(jnp.int32, (rows, 1), 0)
        place = (row % slots).astype(f32)

        def factor(rewards_at, length_at):
            r = jnp.zeros((rows, 1), f32)
            length = jnp.ones((rows, 1), f32)
            for j in range(n):
                mine = row // slots == j
                r = jnp.where(mine, rewards_at(j), r)
                length = jnp.where(mine, length_at(j), length)
            coef = -((r - mean) / spread) / length
            return jnp.where(place < length, coef, 0.0)

        lens = len_ref[...].astype(f32)
        own = factor(lambda j: rew[:, j : j + 1], lambda j: lens[:, j : j + 1])
        other = factor(lambda j: tail[:, j : j + 1], lambda j: tail[:, 2 * n + j : 2 * n + j + 1])
        ds_own[...] = (dval_ref[...].astype(f32) * own).T.astype(bf16)
        ds_other[...] = (got_ref[:, half : half + cols].astype(f32) * other).T.astype(bf16)

    here = pl.ds(pl.multiple_of(pl.program_id(0) * chunk, chunk), chunk)
    acc = jnp.dot(ds_own[...], own_ref[:, here], preferred_element_type=f32)
    acc = acc + jnp.dot(ds_other[...], got_ref[:, here], preferred_element_type=f32)
    for j in range(out_ref.shape[0]):
        out_ref[j] = acc[:, j * LANES : (j + 1) * LANES].astype(bf16)


def sum_kernel(z_ref, got_ref, keep_ref, send_ref):
    total = got_ref[0].astype(f32)
    for s in range(1, got_ref.shape[0]):
        total = total + got_ref[s].astype(f32)
    turned = total.T
    first = z_ref[0] == 0
    keep_ref[...] = jnp.where(first, turned[:BLOCK], turned[BLOCK:])
    send_ref[...] = jnp.where(first, turned[BLOCK:], turned[:BLOCK])


def value_kernel(z_ref, got_ref, own_ref, *refs):
    *parts, v_other_ref, v_own_ref, w_ref = refs
    first = z_ref[0] == 0
    for s, (near, far) in enumerate(zip(parts[:NX], parts[NX:])):
        for y in range(near.shape[0]):
            at = (s * near.shape[0] + y) * 2 * BLOCK
            a, b = near[y].astype(f32), far[y].astype(f32)
            w_ref[at : at + BLOCK] = jnp.where(first, a, b).astype(bf16)
            w_ref[at + BLOCK : at + 2 * BLOCK] = jnp.where(first, b, a).astype(bf16)
    half = w_ref.shape[0]
    v_other_ref[...] = jnp.dot(got_ref[:, :half], w_ref[...], preferred_element_type=f32)
    v_own_ref[...] = jnp.dot(own_ref[...], w_ref[...], preferred_element_type=f32)


def on_chip(array):
    return pltpu.with_memory_space_constraint(array, pltpu.VMEM)


def per_device(resid, norm_gain, w_value, d_value, rewards, lengths):
    rolls, slots, width = resid.shape
    rows = rolls * slots
    cols = w_value.shape[1]
    nx, nz, ny, nc = [lax.axis_size(a) for a in DP]
    half = width // nc
    whole = lambda *shape: pl.BlockSpec(shape, lambda *_: (0,) * len(shape))

    near = lax.ppermute(rewards, "y", Y_PAIR)
    w_y = lax.all_to_all(jnp.broadcast_to(w_value[None], (ny, BLOCK, cols)), "y", 0, 0, tiled=True)
    w_far = lax.ppermute(w_y, "zh", SWAP_Z)
    zpart = lax.axis_index("zh")
    own_w, far_w = [w_y], [w_far]
    for s in range(1, nx):
        own_w.append(lax.ppermute(w_y, "x", X_SHIFTS[s]))
        far_w.append(lax.ppermute(w_far, "x", X_SHIFTS[s]))
    core = lax.axis_index("c").astype(jnp.int32).reshape(1)
    xpos = lax.axis_index("x").astype(jnp.int32).reshape(1)
    zpos = zpart.astype(jnp.int32).reshape(1)
    dval = d_value.reshape(rows, cols)
    rew, near = rewards.reshape(1, rolls), on_chip(near.reshape(1, rolls))
    step = 64
    own, packed = pl.pallas_call(
        norm_kernel,
        grid=(rows // step,),
        in_specs=[
            pl.BlockSpec(memory_space=pltpu.SMEM),
            pl.BlockSpec(memory_space=pltpu.SMEM),
            pl.BlockSpec((step, width), lambda i: (i, 0)),
            whole(1, width),
            pl.BlockSpec((step, cols), lambda i: (i, 0)),
            whole(1, rolls),
            pl.BlockSpec(memory_space=pltpu.VMEM),
            whole(1, rolls),
        ],
        out_specs=[pl.BlockSpec(memory_space=pltpu.VMEM), pl.BlockSpec(memory_space=pltpu.VMEM)],
        out_shape=[pltpu.VMEM((rows, half), bf16), pltpu.VMEM((rows, half + 2 * LANES), bf16)],
        name="norm_split",
    )(core, xpos, resid.reshape(rows, width), norm_gain.reshape(1, width), dval, rew, near, lengths)
    got = lax.ppermute(packed, "c", SWAP)
    got_in, own_in = on_chip(got), on_chip(own)
    send = pl.pallas_call(
        grad_kernel,
        grid_spec=pltpu.PrefetchScalarGridSpec(
            num_scalar_prefetch=1,
            grid=(nx,),
            in_specs=[
                pl.BlockSpec(memory_space=pltpu.VMEM),
                pl.BlockSpec(memory_space=pltpu.VMEM),
                whole(rows, cols),
                whole(1, rolls),
                pl.BlockSpec(memory_space=pltpu.VMEM),
                whole(1, rolls),
            ],
            out_specs=pl.BlockSpec((ny, cols, nz * BLOCK), lambda k, p: ((p[0] + NX - k) % NX, 0, 0)),
            scratch_shapes=[pltpu.VMEM((cols, rows), bf16), pltpu.VMEM((cols, rows), bf16)],
        ),
        out_shape=pltpu.HBM((nx * ny, cols, nz * BLOCK), bf16),
        compiler_params=pltpu.CompilerParams(vmem_limit_bytes=VMEM_GRANT),
        name="grad_partial",
    )(xpos, own_in, got_in, dval, rew, near, lengths)
    g_xy = lax.all_to_all(send, ("x", "y"), 0, 0, tiled=True)
    in_vmem = pl.BlockSpec(memory_space=pltpu.VMEM)
    g_keep, g_send = pl.pallas_call(
        sum_kernel,
        in_specs=[pl.BlockSpec(memory_space=pltpu.SMEM), in_vmem],
        out_specs=[in_vmem, in_vmem],
        out_shape=[pltpu.VMEM((BLOCK, cols), f32), pltpu.VMEM((BLOCK, cols), f32)],
        compiler_params=pltpu.CompilerParams(vmem_limit_bytes=VMEM_GRANT),
        name="grad_sum",
    )(zpos, on_chip(g_xy))
    g_z = lax.ppermute(g_send, "zh", SWAP_Z)
    w_grad = (g_keep + g_z).astype(bf16)

    v_other, v_own = pl.pallas_call(
        value_kernel,
        in_specs=[pl.BlockSpec(memory_space=pltpu.SMEM)] + [in_vmem] * (2 + 2 * nx),
        out_specs=[in_vmem, in_vmem],
        out_shape=[pltpu.VMEM((rows, cols), f32), pltpu.VMEM((rows, cols), f32)],
        scratch_shapes=[pltpu.VMEM((half, cols), bf16)],
        compiler_params=pltpu.CompilerParams(vmem_limit_bytes=VMEM_GRANT),
        name="value_parts",
    )(zpos, got_in, own_in, *[on_chip(w) for w in own_w + far_w])
    v_got = lax.ppermute(v_other, "c", SWAP)
    live = jnp.arange(slots, dtype=jnp.int32)[None, :] < lengths.reshape(rolls, 1)
    value = (v_own + v_got).reshape(rolls, slots, cols) * live.astype(f32)[:, :, None]
    value = value.astype(bf16)
    return value, w_grad


def solution(mesh):
    finer = Mesh(mesh.devices.reshape(4, 2, 8, 2, mesh.shape["tensor"]), DP + ("tensor",))
    placed = (P(DP, None, None), P(), P(DP, "tensor"), P(DP, None, "tensor"), P(DP), P(DP, None))
    return jax.shard_map(
        per_device,
        mesh=finer,
        in_specs=placed,
        out_specs=(P(DP, None, "tensor"), P(DP, "tensor")),
        check_vma=False,
    )
```
